256 devices in a mesh: row: 32 (over z_lo, x, core), col: 8 (over z_hi, y).
Axes of the slice: x: 4, y: 4, z: 8 (z_hi: 2, z_lo: 4; z = z_hi * 4 + z_lo), core: 2. Of those that a mesh axis runs over, the one named last changes fastest.
Arguments:
- right_sides: float32 [16384, 1024], P('row', 'col'), may hold values from -6 to 6
- pencil_s: float32 [16384, 512], P('row'), as said below
- pencil_t: float32 [16384, 512], P('row'), as said below
- value_alpha: float32 [4096], replicated, may hold values from -3 to -0.5
- value_beta: float32 [4096], replicated, may hold values from 0.5 to 1
- selected: int32 [1024], P('col'), may hold values from 0 to 4095
- block_slot: int32 [64], replicated, may hold values from 0 to 63, as said below
- right_basis: float32 [65536, 2, 256], P('row', None, 'col'), may hold values from -0.25 to 0.25
- vectors: float32 [65536, 1024], P('row', 'col'), may hold values from -6 to 6
Outputs:
- updated_sides: float32 [16384, 1024], P('row', 'col')
- updated_vectors: float32 [65536, 1024], P('row', 'col')
The draws below stay inside these ranges and needn't reach their ends.
Inputs may be any that keep to these rules, and one draw needn't show every extreme that they name: A permutation: logical block b of 256 rows is stored at slot block_slot[b]. `pencil_s`: in the window, entries left of the diagonal are 0 and diagonal entries lie in [1, 2]. `pencil_t`: in the window, entries left of the diagonal are 0 and diagonal entries lie in [1, 2].
All inputs are finite; a program needn't handle non-finite values.
Results may differ from the reference program's by a relative error of at most 0.0003.
Values sent between devices are 32-bit elements; how exact they have to be, the bound alone decides.
A program may use at most 64 MiB of HBM per device.

```python
import jax
import jax.numpy as jnp
from jax import lax

NEIG = 1024
BLK = 256
ORDER = 65536
POOL = 4096
LEAD = 16384
NBLK = 64
WIN = 512


def slot_order(key):
    return jax.random.permutation(jax.random.fold_in(key, 11), NBLK).astype(jnp.int32)


def draw_block_slot(key, part):
    return slot_order(key)


def pencil_factor(key, salt):
    base_key = jax.random.fold_in(key, salt)
    rough_key, diag_key = jax.random.split(base_key)
    width = 2 * BLK
    lead_rows = NBLK * BLK
    rough = jax.random.normal(rough_key, (lead_rows, width), jnp.float32)
    diagonal = jax.random.uniform(diag_key, (lead_rows, width), jnp.float32, 1.0, 2.0)
    row_index = jax.lax.broadcasted_iota(jnp.int32, (lead_rows, width), 0)
    col_index = jax.lax.broadcasted_iota(jnp.int32, (lead_rows, width), 1)
    window_row = row_index - (lead_rows - width)
    inside = jnp.where(col_index > window_row, rough * (0.6 / width ** 0.5), jnp.where(col_index == window_row, diagonal, 0.0))
    logical = jnp.where(window_row >= 0, inside, rough * (1.0 / width ** 0.5))
    stored = jnp.zeros((NBLK, BLK, width), jnp.float32).at[slot_order(key)].set(logical.reshape(NBLK, BLK, width))
    return stored.reshape(lead_rows, width)


def draw_pencil_s(key, part):
    return pencil_factor(key, 21)


def draw_pencil_t(key, part):
    return pencil_factor(key, 22)


def set_ends(result, stream_key, smallest, top_value):
    dims = result.shape
    place = [jax.random.randint(jax.random.fold_in(stream_key, axis), (), 0, dims[axis]) for axis in range(len(dims))]
    result = result.at[tuple(place)].set(smallest)
    longest = dims.index(max(dims))
    place[longest] = (place[longest] + 1) % dims[longest]
    return result.at[tuple(place)].set(top_value)


def steps_of(own_key, dims, shards, low, top_value):
    level, own = 1.0, jax.random.fold_in(own_key, 6)
    for position, blocks in shards:
        heights = jnp.exp(jax.random.uniform(jax.random.fold_in(own, position), (blocks,), jnp.float32, low / len(shards), top_value / len(shards)))
        level = level * jnp.repeat(heights, dims[position] // blocks).reshape([-1 if axis == position else 1 for axis in range(len(dims))])
    return level


def gaussian(own_key, extent, scale, reach, cuts=(), kind=jnp.bfloat16):
    array = scale * jax.random.normal(own_key, extent, jnp.float32)
    if cuts:
        array = array * steps_of(own_key, extent, cuts, -0.22, 0.18)
    return jnp.clip(array, -reach, reach).astype(kind)


def setup_inputs(seed: int = 0) -> dict:
    seeds = jax.random.split(jax.random.key(seed), 10)
    return {
        "right_sides": gaussian(seeds[0], (LEAD, NEIG), 1.0, 6.0, ((0, 32), (1, 8)), jnp.float32),
        "pencil_s": draw_pencil_s(jax.random.fold_in(seeds[9], 71), 0),
        "pencil_t": draw_pencil_t(jax.random.fold_in(seeds[9], 71), 0),
        "value_alpha": jnp.clip(jax.random.uniform(seeds[3], (POOL,), jnp.float32, -3.0, -0.5), -3.0, -0.5),
        "value_beta": jnp.clip(jax.random.uniform(seeds[4], (POOL,), jnp.float32, 0.5, 1.0), 0.5, 1.0),
        "selected": set_ends(jax.random.randint(seeds[5], (NEIG,), 0, POOL), jax.random.fold_in(seeds[5], 1), 0, POOL - 1).astype(jnp.int32),
        "block_slot": draw_block_slot(jax.random.fold_in(seeds[9], 71), 0),
        "right_basis": gaussian(seeds[7], (ORDER, 2, BLK), WIN ** -0.5, 0.25, ((0, 32), (2, 8)), jnp.float32),
        "vectors": gaussian(seeds[8], (ORDER, NEIG), 1.0, 6.0, ((0, 32), (1, 8)), jnp.float32),
    }


def reference(right_sides, pencil_s, pencil_t, value_alpha, value_beta, selected, block_slot, right_basis, vectors):
    exact_mode = lax.Precision.HIGHEST
    shift_alpha = value_alpha[selected]
    shift_beta = value_beta[selected]
    block_count = block_slot.shape[0]
    width = 2 * BLK
    lead_rows = block_count * BLK
    logical_s = pencil_s.reshape(block_count, BLK, width)[block_slot].reshape(lead_rows, width)
    logical_t = pencil_t.reshape(block_count, BLK, width)[block_slot].reshape(lead_rows, width)
    logical_r = right_sides.reshape(block_count, BLK, NEIG)[block_slot].reshape(lead_rows, NEIG)
    window_s = logical_s[lead_rows - width:]
    window_t = logical_t[lead_rows - width:]
    window_r = logical_r[lead_rows - width:]
    index_rows = jnp.arange(width, dtype=jnp.int32)

    def back_step(pending, column):
        s_column = lax.dynamic_index_in_dim(window_s, column, 1, keepdims=False)
        t_column = lax.dynamic_index_in_dim(window_t, column, 1, keepdims=False)
        pivot_value = shift_beta * s_column[column] - shift_alpha * t_column[column]
        solved = pending[column] / pivot_value
        s_masked = jnp.where(index_rows < column, s_column, 0.0)
        t_masked = jnp.where(index_rows < column, t_column, 0.0)
        pending = pending - (s_masked[:, None] * (shift_beta * solved)[None, :] - t_masked[:, None] * (shift_alpha * solved)[None, :])
        return pending, solved

    steps_down = jnp.arange(width - 1, -1, -1, dtype=jnp.int32)
    _, solved_rows = lax.scan(back_step, window_r, steps_down)
    window_x = solved_rows[::-1]
    update = jnp.dot(logical_s, window_x * shift_beta[None, :], precision=exact_mode, preferred_element_type=jnp.float32)
    update = update - jnp.dot(logical_t, window_x * shift_alpha[None, :], precision=exact_mode, preferred_element_type=jnp.float32)
    new_sides = (logical_r - update).at[lead_rows - width:].set(window_x)
    stored = jnp.zeros((block_count, BLK, NEIG), new_sides.dtype).at[block_slot].set(new_sides.reshape(block_count, BLK, NEIG))
    updated_sides = stored.reshape(lead_rows, NEIG)
    basis = right_basis.reshape(ORDER, width)
    updated_vectors = vectors + jnp.dot(basis, window_x, precision=exact_mode, preferred_element_type=jnp.float32)
    return (updated_sides, updated_vectors)
```

```python
import functools

import jax
import jax.numpy as jnp
from jax import lax
from jax.experimental import pallas as pl
from jax.experimental.pallas import tpu as pltpu
from jax.sharding import PartitionSpec as P

MESH = pl.DeviceIdType.MESH
BLK = 256
SUB = 32
PANELS = BLK // SUB
NCH = 8
CH = 64 // NCH
ORD = 2048
F32 = jnp.float32
BF = jnp.bfloat16
FIRST_Z = 3


def split(v):
    hi = v.astype(BF)
    return hi, (v - hi.astype(F32)).astype(BF)


def dot(a, b):
    return jnp.dot(a, b, preferred_element_type=F32)


def dot3(a, b):
    ah, al = split(a)
    bh, bl = split(b)
    return dot(ah, bh) + (dot(ah, bl) + dot(al, bh))


def kernel(
    slot_ref, alpha_ref, beta_ref, sel_ref, side_hbm, s_hbm, t_hbm, zt,
    out_side, out_vec,
    side_ref, s_ref, t_ref, zbuf, sd, td, lmat, rbuf, cand, st1, st2, xw, xpad, coef, shifts,
    zr, zs, s1r, s1s, s2r, s2s, s3r, s3s, lsem,
):
    row = lax.axis_index("row")
    col = lax.axis_index("col")
    zlo = row // 8
    pi = row % 8
    zh = col // 4
    y = col % 4
    yp, ym, y2 = (y + 1) % 4, (y + 3) % 4, (y + 2) % 4
    oh = 1 - zh

    loads = []
    for n, (src, dst) in enumerate(((s_hbm, s_ref), (t_hbm, t_ref), (side_hbm, side_ref), (zt, zbuf.at[col]))):
        loads.append(pltpu.make_async_copy(src, dst, lsem.at[n]))
        loads[-1].start()

    bar = pltpu.get_barrier_semaphore()
    peers = [(row, zh * 4 + yp), (row, zh * 4 + ym), (row, oh * 4 + y)]
    peers += [(zlo * 8 + (pi + d) % 8, col) for d in range(1, 8)]
    peers += [(((zlo + d) % 4) * 8 + pi, col) for d in range(1, 4)]
    for d in peers:
        pl.semaphore_signal(bar, inc=1, device_id=d, device_id_type=MESH)
    pl.semaphore_wait(bar, len(peers))

    zsends = []

    def piece(p, k):
        return zbuf.at[p, pl.ds(k * CH, CH)]

    def zsend(src, p, k, dcol):
        n = len(zsends)
        c = pltpu.make_async_remote_copy(
            src_ref=src, dst_ref=piece(p, k), send_sem=zs.at[n], recv_sem=zr.at[p, k],
            device_id=(row, dcol), device_id_type=MESH,
        )
        c.start()
        zsends.append(c)

    def zwait(p, k):
        pltpu.make_async_copy(piece(p, k), piece(p, k), zr.at[p, k]).wait()

    def own(k):
        return zt.at[pl.ds(k * CH, CH)]

    cp, cm, c2 = zh * 4 + yp, zh * 4 + ym, zh * 4 + y2
    q, qp, qm, q2 = oh * 4 + y, oh * 4 + yp, oh * 4 + ym, oh * 4 + y2

    def send_z(ks):
        for k in ks:
            zsend(own(k), col, k, q)

    def send_own():
        for k in range(NCH):
            zsend(own(k), col, k, cp)
            zsend(own(k), col, k, cm)

    def forward_own(ks):
        for k in ks:
            if k % 2 == 0:
                zwait(cm, k)
                zsend(piece(cm, k), cm, k, cp)
            else:
                zwait(cp, k)
                zsend(piece(cp, k), cp, k, cm)

    def send_far(ks):
        for k in ks:
            zwait(q, k)
            zsend(piece(q, k), q, k, cp)
            zsend(piece(q, k), q, k, cm)

    def forward_far(ks):
        for k in ks:
            if k % 2 == 0:
                zwait(qm, k)
                zsend(piece(qm, k), qm, k, cp)
            else:
                zwait(qp, k)
                zsend(piece(qp, k), qp, k, cm)

    send_z(range(FIRST_Z))
    send_own()

    sel = sel_ref[...]
    hot = (lax.broadcasted_iota(jnp.int32, (128, 128), 0) == sel % 128).astype(F32)
    rows_hot = lax.broadcasted_iota(jnp.int32, (32, 128), 0) == sel // 128

    def lookup(table):
        got = jnp.dot(table, hot, precision=lax.Precision.HIGHEST, preferred_element_type=F32)
        return jnp.sum(jnp.where(rows_hot, got, 0.0), axis=0, keepdims=True)

    shifts[0:1] = lookup(alpha_ref[...])
    shifts[1:2] = lookup(beta_ref[...])
    alpha = shifts[0:1]
    beta = shifts[1:2]

    slots = [slot_ref[0:1, 63:64], slot_ref[0:1, 62:63]]

    def half(ref, w, lanes):
        odd = jnp.broadcast_to(slots[w] % 2 == 1, (BLK, lanes.stop - lanes.start))
        return jnp.where(odd, ref[BLK:, lanes], ref[:BLK, lanes])

    def pick(ref, w, which, count):
        got = ref[w, 0]
        for i in range(1, count):
            got = jnp.where(jnp.broadcast_to(which == i, (SUB, 128)), ref[w, i], got)
        return got

    def prepare(w):
        cols = slice(BLK, 2 * BLK) if w == 0 else slice(0, BLK)
        s_diag = half(s_ref, w, cols)
        t_diag = half(t_ref, w, cols)
        sd[...] = s_diag
        td[...] = t_diag
        s_hi, s_lo = split(s_diag)
        t_hi, t_lo = split(t_diag)
        for g in range(2):
            c = slice(g * 128, g * 128 + 128)
            lmat[g, 0:256, 0:128] = s_hi[:, c]
            lmat[g, 0:256, 128:256] = t_hi[:, c]
            lmat[g, 256:512, 0:128] = s_lo[:, c]
            lmat[g, 256:512, 128:256] = t_lo[:, c]
        rbuf[...] = half(side_ref, w, slice(0, 128))

    lane = lax.broadcasted_iota(jnp.int32, (SUB, 128), 1)
    subl = lax.broadcasted_iota(jnp.int32, (SUB, 128), 0)

    def solve(w):
        xpad[...] = jnp.zeros_like(xpad)

        def panel(t, _):
            p = PANELS - 1 - t
            r0 = pl.multiple_of(p * SUB, SUB)
            g = p // 4
            off = pl.multiple_of((p % 4) * SUB, SUB)
            lanes = pl.ds(pl.multiple_of(g * 128, 128), 128)
            turn = (128 - off) % 128
            s_rows = pltpu.roll(sd[pl.ds(r0, SUB), lanes], turn, 1)
            t_rows = pltpu.roll(td[pl.ds(r0, SUB), lanes], turn, 1)
            on_diag = lane == subl
            s_d = jnp.sum(jnp.where(on_diag, s_rows, 0.0), axis=1, keepdims=True)
            t_d = jnp.sum(jnp.where(on_diag, t_rows, 0.0), axis=1, keepdims=True)
            inv = 1.0 / (beta * s_d - alpha * t_d)
            for j in range(1, SUB):
                h = 8 * (j // 8 + 1)
                c_j = beta * s_rows[0:h, j:j + 1] - alpha * t_rows[0:h, j:j + 1]
                coef[j, 0:h] = jnp.where(subl[0:h] < j, c_j * inv[j:j + 1], 0.0)
            r = [rbuf[pl.ds(r0 + 8 * i, 8), :] for i in range(4)]
            for j in reversed(range(1, SUB)):
                i = j // 8
                entry = jnp.broadcast_to(r[i][j % 8:j % 8 + 1], (8, 128))
                for a in range(i + 1):
                    r[a] = r[a] - coef[j, 8 * a:8 * a + 8] * entry
            x_p = jnp.concatenate(r, 0) * inv
            cand[w, pl.ds(r0, SUB)] = x_p

            @pl.when(p != pi)
            def _():
                stage1(w, p).start()

            @pl.when(p == pi)
            def _():
                st1[w, pi] = x_p

            xpad[pl.ds(off, SUB)] = beta * x_p
            xpad[pl.ds(128 + off, SUB)] = -(alpha * x_p)
            hi, lo = split(xpad[...])
            prod = dot(lmat[g], jnp.concatenate([hi, lo], 1))
            rbuf[...] -= prod[0:256, 0:128] + (prod[0:256, 128:256] + prod[256:512, 0:128])
            xpad[pl.ds(off, SUB)] = jnp.zeros((SUB, 128), F32)
            xpad[pl.ds(128 + off, SUB)] = jnp.zeros((SUB, 128), F32)
            return 0

        lax.fori_loop(0, PANELS, panel, 0)

    def stage1(w, p):
        return pltpu.make_async_remote_copy(
            src_ref=cand.at[w, pl.ds(pl.multiple_of(p * SUB, SUB), SUB)], dst_ref=st1.at[w, pi],
            send_sem=s1s.at[w, p], recv_sem=s1r.at[w, pi],
            device_id=(zlo * 8 + p, col), device_id_type=MESH,
        )

    def stage2(w):
        owner = slots[w] // 2
        for d in range(1, 8):
            src = (pi + d) % 8
            pltpu.make_async_copy(st1.at[w, src], st1.at[w, src], s1r.at[w, src]).wait()
        st2[w, zlo] = pick(st1, w, owner % 8, 8)
        for d in range(1, 4):
            pltpu.make_async_remote_copy(
                src_ref=st2.at[w, zlo], dst_ref=st2.at[w, zlo],
                send_sem=s2s.at[w, d], recv_sem=s2r.at[w, zlo],
                device_id=(((zlo + d) % 4) * 8 + pi, col), device_id_type=MESH,
            ).start()

    def mine():
        return pl.ds(pl.multiple_of(pi * SUB, SUB), SUB)

    def stage3(w):
        owner = slots[w] // 2
        for d in range(1, 4):
            src = (zlo + d) % 4
            pltpu.make_async_copy(st2.at[w, src], st2.at[w, src], s2r.at[w, src]).wait()
        xw[w, mine()] = pick(st2, w, owner // 8, 4)
        for d in range(1, 8):
            pltpu.make_async_remote_copy(
                src_ref=xw.at[w, mine()], dst_ref=xw.at[w, mine()],
                send_sem=s3s.at[w, d], recv_sem=s3r.at[w, pi],
                device_id=(zlo * 8 + (pi + d) % 8, col), device_id_type=MESH,
            ).start()

    def stage4(w):
        for d in range(1, 8):
            src = (pi + d) % 8
            part = xw.at[w, pl.ds(pl.multiple_of(src * SUB, SUB), SUB)]
            pltpu.make_async_copy(part, part, s3r.at[w, src]).wait()

    def drain(w):
        for d in range(1, 8):
            p = (pi + d) % 8
            stage1(w, p).wait_send()
            pltpu.make_async_copy(xw.at[w, mine()], xw.at[w, mine()], s3s.at[w, d]).wait()
        for d in range(1, 4):
            pltpu.make_async_copy(st2.at[w, zlo], st2.at[w, zlo], s2s.at[w, d]).wait()

    def apply(s_cols, t_cols, x):
        return dot3(s_cols, beta * x) - dot3(t_cols, alpha * x)

    for c in loads[:3]:
        c.wait()
    prepare(0)
    solve(0)
    stage2(0)
    send_z(range(FIRST_Z, NCH))
    forward_own(range(NCH))
    prepare(1)
    stage3(0)
    send_far(range(FIRST_Z))
    stage4(0)

    right = slice(BLK, 2 * BLK)
    rbuf[...] -= apply(half(s_ref, 1, right), half(t_ref, 1, right), xw[0])
    solve(1)
    stage2(1)
    send_far(range(FIRST_Z, NCH))
    for h in range(2):
        rs = slice(h * BLK, h * BLK + BLK)
        out_side[rs, :] = side_ref[rs, :] - apply(s_ref[rs, BLK:], t_ref[rs, BLK:], xw[0])
    stage3(1)
    forward_far(range(NCH))
    stage4(1)

    for h in range(2):
        rs = slice(h * BLK, h * BLK + BLK)
        new = out_side[rs, :] - apply(s_ref[rs, :BLK], t_ref[rs, :BLK], xw[1])
        here = row * 2 + h
        new = jnp.where(jnp.broadcast_to(slots[1] == here, (BLK, 128)), xw[1], new)
        out_side[rs, :] = jnp.where(jnp.broadcast_to(slots[0] == here, (BLK, 128)), xw[0], new)

    loads[3].wait()

    def product(c, first):
        at = pl.ds(pl.multiple_of(c * SUB, SUB), SUB)
        x = jnp.concatenate([xw[1, at], xw[0, at]], 0)
        xh, xl = split(x)
        xs = jnp.concatenate([xh, xl, xh], 0)

        def chunk(m, _):
            rows = pl.ds(pl.multiple_of(m * 256, 256), 256)
            zh_, zl_ = split(zbuf[c, :, rows])
            zz = jnp.concatenate([zh_, zh_, zl_], 0)
            part = lax.dot_general(zz, xs, (((0,), (0,)), ((), ())), preferred_element_type=F32)
            out_vec[rows, :] = part if first else out_vec[rows, :] + part
            return 0

        lax.fori_loop(0, ORD // 256, chunk, 0)

    product(col, True)
    for k in range(NCH):
        zwait(cp if k % 2 == 0 else cm, k)
    product(cp, False)
    product(cm, False)
    for k in range(NCH):
        zwait(c2, k)
    product(c2, False)
    product(q, False)
    for k in range(NCH):
        zwait(qp if k % 2 == 0 else qm, k)
    product(qp, False)
    product(qm, False)
    for k in range(NCH):
        zwait(q2, k)
    product(q2, False)
    for c in zsends:
        c.wait_send()
    drain(0)
    drain(1)


def on_device(right_sides, pencil_s, pencil_t, value_alpha, value_beta, selected, block_slot, right_basis, vectors):
    zt = right_basis.transpose(1, 2, 0).reshape(64, ORD)
    vm = pl.BlockSpec(memory_space=pltpu.VMEM)
    dma = pltpu.SemaphoreType.DMA
    sides, prod = pl.pallas_call(
        kernel,
        out_shape=(jax.ShapeDtypeStruct((512, 128), F32), jax.ShapeDtypeStruct((ORD, 128), F32)),
        in_specs=[vm] * 4 + [pl.BlockSpec(memory_space=pl.ANY)] * 4,
        out_specs=(vm, vm),
        scratch_shapes=[
            pltpu.VMEM((512, 128), F32),
            pltpu.VMEM((512, 512), F32),
            pltpu.VMEM((512, 512), F32),
            pltpu.VMEM((8, 64, ORD), F32),
            pltpu.VMEM((BLK, BLK), F32),
            pltpu.VMEM((BLK, BLK), F32),
            pltpu.VMEM((2, 512, 256), BF),
            pltpu.VMEM((BLK, 128), F32),
            pltpu.VMEM((2, BLK, 128), F32),
            pltpu.VMEM((2, 8, SUB, 128), F32),
            pltpu.VMEM((2, 4, SUB, 128), F32),
            pltpu.VMEM((2, BLK, 128), F32),
            pltpu.VMEM((256, 128), F32),
            pltpu.VMEM((SUB, SUB, 128), F32),
            pltpu.VMEM((8, 128), F32),
            dma((8, NCH)), dma((7 * NCH,)),
            dma((2, 8)), dma((2, 8)), dma((2, 4)), dma((2, 4)), dma((2, 8)), dma((2, 8)),
            dma((4,)),
        ],
        compiler_params=pltpu.CompilerParams(
            collective_id=0, has_side_effects=True, vmem_limit_bytes=60 << 20
        ),
    )(
        block_slot.reshape(1, 64), value_alpha.reshape(32, 128), value_beta.reshape(32, 128),
        selected.reshape(1, 128), right_sides, pencil_s, pencil_t, zt,
    )
    return sides, vectors + prod


def solution(mesh):
    return jax.shard_map(
        on_device,
        mesh=mesh,
        in_specs=(
            P("row", "col"), P("row", None), P("row", None), P(), P(), P("col"), P(),
            P("row", None, "col"), P("row", "col"),
        ),
        out_specs=(P("row", "col"), P("row", "col")),
        check_vma=False,
    )
```

```python
import functools

import jax
import jax.numpy as jnp
from jax import lax
from jax.experimental import pallas as pl
from jax.experimental.pallas import tpu as pltpu
from jax.sharding import PartitionSpec as P

MESH = pl.DeviceIdType.MESH
BLK = 256
SUB = 32
PANELS = BLK // SUB
NCH = 8
CH = 64 // NCH
ORD = 2048
F32 = jnp.float32
BF = jnp.bfloat16
Z_A = 2
Z_B = 6


def split(v):
    hi = v.astype(BF)
    return hi, (v - hi.astype(F32)).astype(BF)


def dot(a, b):
    return jnp.dot(a, b, preferred_element_type=F32)


def kernel(
    slot_ref, alpha_ref, beta_ref, sel_ref, side_hbm, s_hbm, t_hbm, zt,
    out_side, out_vec,
    side_ref, s_ref, t_ref, zbuf, zhi, zlow, sd, td, lmat, rbuf, cand, st1, st2, xw, xpad, coef, shifts,
    zr, zs, s1r, s1s, s2r, s2s, s3r, s3s, lsem,
):
    row = lax.axis_index("row")
    col = lax.axis_index("col")
    zlo = row // 8
    pi = row % 8
    zh = col // 4
    y = col % 4
    yp, ym, y2 = (y + 1) % 4, (y + 3) % 4, (y + 2) % 4
    oh = 1 - zh

    loads = []
    for n, (src, dst) in enumerate(((s_hbm, s_ref), (t_hbm, t_ref), (side_hbm, side_ref), (zt, zbuf.at[col]))):
        loads.append(pltpu.make_async_copy(src, dst, lsem.at[n]))
        loads[-1].start()

    bar = pltpu.get_barrier_semaphore()
    peers = [(row, zh * 4 + yp), (row, zh * 4 + ym), (row, oh * 4 + y)]
    peers += [(zlo * 8 + (pi + d) % 8, col) for d in range(1, 8)]
    peers += [(((zlo + d) % 4) * 8 + pi, col) for d in range(1, 4)]
    for d in peers:
        pl.semaphore_signal(bar, inc=1, device_id=d, device_id_type=MESH)
    pl.semaphore_wait(bar, len(peers))

    zsends = []

    def piece(p, k):
        return zbuf.at[p, pl.ds(k * CH, CH)]

    def zsend(src, p, k, dcol):
        n = len(zsends)
        c = pltpu.make_async_remote_copy(
            src_ref=src, dst_ref=piece(p, k), send_sem=zs.at[n], recv_sem=zr.at[p, k],
            device_id=(row, dcol), device_id_type=MESH,
        )
        c.start()
        zsends.append((p, k))

    def zwait(p, k):
        pltpu.make_async_copy(piece(p, k), piece(p, k), zr.at[p, k]).wait()

    def own(k):
        return zt.at[pl.ds(k * CH, CH)]

    cp, cm, c2 = zh * 4 + yp, zh * 4 + ym, zh * 4 + y2
    q, qp, qm, q2 = oh * 4 + y, oh * 4 + yp, oh * 4 + ym, oh * 4 + y2

    def send_z(ks):
        for k in ks:
            zsend(own(k), col, k, q)

    def send_own():
        for k in range(NCH):
            zsend(own(k), col, k, cp)
            zsend(own(k), col, k, cm)

    def forward_own(ks):
        for k in ks:
            if k % 2 == 0:
                zwait(cm, k)
                zsend(piece(cm, k), cm, k, cp)
            else:
                zwait(cp, k)
                zsend(piece(cp, k), cp, k, cm)

    def send_far(ks):
        for k in ks:
            zwait(q, k)
            zsend(piece(q, k), q, k, cp)
            zsend(piece(q, k), q, k, cm)

    def forward_far(ks):
        for k in ks:
            if k % 2 == 0:
                zwait(qm, k)
                zsend(piece(qm, k), qm, k, cp)
            else:
                zwait(qp, k)
                zsend(piece(qp, k), qp, k, cm)

    send_z(range(Z_A))
    send_own()

    sel = sel_ref[...]
    hot = (lax.broadcasted_iota(jnp.int32, (128, 128), 0) == sel % 128).astype(F32)
    rows_hot = lax.broadcasted_iota(jnp.int32, (32, 128), 0) == sel // 128

    def lookup(table):
        got = jnp.dot(table, hot, precision=lax.Precision.HIGHEST, preferred_element_type=F32)
        return jnp.sum(jnp.where(rows_hot, got, 0.0), axis=0, keepdims=True)

    shifts[0:1] = lookup(alpha_ref[...])
    shifts[1:2] = lookup(beta_ref[...])
    alpha = shifts[0:1]
    beta = shifts[1:2]

    slots = [slot_ref[0:1, 63:64], slot_ref[0:1, 62:63]]

    def half(ref, w, lanes):
        odd = jnp.broadcast_to(slots[w] % 2 == 1, (BLK, lanes.stop - lanes.start))
        return jnp.where(odd, ref[BLK:, lanes], ref[:BLK, lanes])

    def pick(ref, w, which, count):
        got = ref[w, 0]
        for i in range(1, count):
            got = jnp.where(jnp.broadcast_to(which == i, (SUB, 128)), ref[w, i], got)
        return got

    def prepare(w):
        cols = slice(BLK, 2 * BLK) if w == 0 else slice(0, BLK)
        s_diag = half(s_ref, w, cols)
        t_diag = half(t_ref, w, cols)
        sd[...] = s_diag
        td[...] = t_diag
        s_hi, s_lo = split(s_diag)
        t_hi, t_lo = split(t_diag)
        for g in range(2):
            c = slice(g * 128, g * 128 + 128)
            lmat[g, 0:256, 0:128] = s_hi[:, c]
            lmat[g, 0:256, 128:256] = t_hi[:, c]
            lmat[g, 256:512, 0:128] = s_lo[:, c]
            lmat[g, 256:512, 128:256] = t_lo[:, c]
        rbuf[...] = half(side_ref, w, slice(0, 128))

    lane = lax.broadcasted_iota(jnp.int32, (SUB, 128), 1)
    subl = lax.broadcasted_iota(jnp.int32, (SUB, 128), 0)

    def solve(w, hooks):
        xpad[...] = jnp.zeros_like(xpad)

        def panel(t, _):
            for at, hook in hooks.items():
                pl.when(t == at)(hook)
            p = PANELS - 1 - t
            r0 = pl.multiple_of(p * SUB, SUB)
            g = p // 4
            off = pl.multiple_of((p % 4) * SUB, SUB)
            lanes = pl.ds(pl.multiple_of(g * 128, 128), 128)
            turn = (128 - off) % 128
            s_rows = pltpu.roll(sd[pl.ds(r0, SUB), lanes], turn, 1)
            t_rows = pltpu.roll(td[pl.ds(r0, SUB), lanes], turn, 1)
            on_diag = lane == subl
            s_d = jnp.sum(jnp.where(on_diag, s_rows, 0.0), axis=1, keepdims=True)
            t_d = jnp.sum(jnp.where(on_diag, t_rows, 0.0), axis=1, keepdims=True)
            inv = 1.0 / (beta * s_d - alpha * t_d)
            for j in range(1, SUB):
                h = 8 * (j // 8 + 1)
                c_j = beta * s_rows[0:h, j:j + 1] - alpha * t_rows[0:h, j:j + 1]
                coef[j, 0:h] = jnp.where(subl[0:h] < j, c_j * inv[j:j + 1], 0.0)
            r = [rbuf[pl.ds(r0 + 8 * i, 8), :] for i in range(4)]
            for j in reversed(range(1, SUB)):
                i = j // 8
                entry = jnp.broadcast_to(r[i][j % 8:j % 8 + 1], (8, 128))
                for a in range(i + 1):
                    r[a] = r[a] - coef[j, 8 * a:8 * a + 8] * entry
            x_p = jnp.concatenate(r, 0) * inv
            cand[w, pl.ds(r0, SUB)] = x_p

            @pl.when(p != pi)
            def _():
                stage1(w, p).start()

            @pl.when(p == pi)
            def _():
                st1[w, pi] = x_p

            xpad[pl.ds(off, SUB)] = beta * x_p
            xpad[pl.ds(128 + off, SUB)] = -(alpha * x_p)
            hi, lo = split(xpad[...])
            prod = dot(lmat[g], jnp.concatenate([hi, lo], 1))
            rbuf[...] -= prod[0:256, 0:128] + (prod[0:256, 128:256] + prod[256:512, 0:128])
            xpad[pl.ds(off, SUB)] = jnp.zeros((SUB, 128), F32)
            xpad[pl.ds(128 + off, SUB)] = jnp.zeros((SUB, 128), F32)
            return 0

        lax.fori_loop(0, PANELS, panel, 0)

    def stage1(w, p):
        return pltpu.make_async_remote_copy(
            src_ref=cand.at[w, pl.ds(pl.multiple_of(p * SUB, SUB), SUB)], dst_ref=st1.at[w, pi],
            send_sem=s1s.at[w, p], recv_sem=s1r.at[w, pi],
            device_id=(zlo * 8 + p, col), device_id_type=MESH,
        )

    def stage2(w):
        owner = slots[w] // 2
        for d in range(1, 8):
            src = (pi + d) % 8
            pltpu.make_async_copy(st1.at[w, src], st1.at[w, src], s1r.at[w, src]).wait()
        st2[w, zlo] = pick(st1, w, owner % 8, 8)
        for d in range(1, 4):
            pltpu.make_async_remote_copy(
                src_ref=st2.at[w, zlo], dst_ref=st2.at[w, zlo],
                send_sem=s2s.at[w, d], recv_sem=s2r.at[w, zlo],
                device_id=(((zlo + d) % 4) * 8 + pi, col), device_id_type=MESH,
            ).start()

    def mine():
        return pl.ds(pl.multiple_of(pi * SUB, SUB), SUB)

    def stage3(w):
        owner = slots[w] // 2
        for d in range(1, 4):
            src = (zlo + d) % 4
            pltpu.make_async_copy(st2.at[w, src], st2.at[w, src], s2r.at[w, src]).wait()
        xw[w, mine()] = pick(st2, w, owner // 8, 4)
        for d in range(1, 8):
            pltpu.make_async_remote_copy(
                src_ref=xw.at[w, mine()], dst_ref=xw.at[w, mine()],
                send_sem=s3s.at[w, d], recv_sem=s3r.at[w, pi],
                device_id=(zlo * 8 + (pi + d) % 8, col), device_id_type=MESH,
            ).start()

    def stage4(w):
        for d in range(1, 8):
            src = (pi + d) % 8
            part = xw.at[w, pl.ds(pl.multiple_of(src * SUB, SUB), SUB)]
            pltpu.make_async_copy(part, part, s3r.at[w, src]).wait()

    def drain(w):
        for d in range(1, 8):
            p = (pi + d) % 8
            stage1(w, p).wait_send()
            pltpu.make_async_copy(xw.at[w, mine()], xw.at[w, mine()], s3s.at[w, d]).wait()
        for d in range(1, 4):
            pltpu.make_async_copy(st2.at[w, zlo], st2.at[w, zlo], s2s.at[w, d]).wait()

    def apply(s_cols, t_cols, x):
        lh, ll = split(jnp.concatenate([s_cols, t_cols], 1))
        rh, rl = split(jnp.concatenate([beta * x, -(alpha * x)], 0))
        wide = dot(lh, jnp.concatenate([rh, rl], 1))
        return wide[:, 0:128] + (wide[:, 128:256] + dot(ll, rh))

    order = [col, cp, cm, c2, q, qp, qm, q2]

    def convert(pair):
        first, second = order[2 * pair], order[2 * pair + 1]

        def chunk(m, _):
            rows = pl.ds(pl.multiple_of(m * 256, 256), 256)
            both = jnp.concatenate([zbuf[first, :, rows], zbuf[second, :, rows]], 0)
            hi, lo = split(both.T)
            zhi[rows, 128 * pair:128 * pair + 128] = hi
            zlow[rows, 128 * pair:128 * pair + 128] = lo
            return 0

        lax.fori_loop(0, ORD // 256, chunk, 0)

    def product(pairs, first):
        xs = []
        for c in order[2 * pairs[0]:2 * pairs[-1] + 2]:
            at = pl.ds(pl.multiple_of(c * SUB, SUB), SUB)
            xs += [xw[1, at], xw[0, at]]
        xh, xl = split(jnp.concatenate(xs, 0))
        wide_x = jnp.concatenate([xh, xl], 1)
        ks = slice(128 * pairs[0], 128 * pairs[-1] + 128)

        def chunk(m, _):
            rows = pl.ds(pl.multiple_of(m * 256, 256), 256)
            wide = dot(zhi[rows, ks], wide_x)
            part = wide[:, 0:128] + (wide[:, 128:256] + dot(zlow[rows, ks], xh))
            out_vec[rows, :] = part if first else out_vec[rows, :] + part
            return 0

        lax.fori_loop(0, ORD // 256, chunk, 0)

    right = slice(BLK, 2 * BLK)
    for c in loads[:3]:
        c.wait()
    prepare(0)
    solve(0, {})
    stage2(0)
    forward_own(range(0, 4))
    prepare(1)
    stage3(0)
    send_z(range(Z_A, Z_B))
    send_far(range(Z_A))
    stage4(0)
    rbuf[...] -= apply(half(s_ref, 1, right), half(t_ref, 1, right), xw[0])
    hooks = {0: lambda: forward_own([4, 5]), 2: lambda: forward_own([6, 7])}
    hooks[5] = lambda: send_far([Z_A])
    solve(1, hooks)
    stage2(1)
    send_far(range(Z_A + 1, Z_B))
    forward_far(range(0, Z_A))
    for h in range(2):
        rs = slice(h * BLK, h * BLK + BLK)
        out_side[rs, :] = side_ref[rs, :] - apply(s_ref[rs, BLK:], t_ref[rs, BLK:], xw[0])
    loads[3].wait()
    stage3(1)
    send_z(range(Z_B, NCH))
    for k in range(NCH):
        zwait(cp if k % 2 == 0 else cm, k)
    convert(0)
    forward_far(range(Z_A, Z_B - 1))
    for k in range(NCH):
        zwait(c2, k)
    convert(1)
    forward_far(range(Z_B - 1, Z_B))
    stage4(1)
    send_far(range(Z_B, NCH))
    product([0, 1], True)

    for h in range(2):
        rs = slice(h * BLK, h * BLK + BLK)
        new = out_side[rs, :] - apply(s_ref[rs, :BLK], t_ref[rs, :BLK], xw[1])
        here = row * 2 + h
        new = jnp.where(jnp.broadcast_to(slots[1] == here, (BLK, 128)), xw[1], new)
        out_side[rs, :] = jnp.where(jnp.broadcast_to(slots[0] == here, (BLK, 128)), xw[0], new)

    forward_far(range(Z_B, NCH))
    for k in range(NCH):
        zwait(qp if k % 2 == 0 else qm, k)
    convert(2)
    product([2], False)
    for k in range(NCH):
        zwait(q2, k)
    convert(3)
    product([3], False)
    for n, (p, k) in enumerate(zsends):
        pltpu.make_async_copy(piece(p, k), piece(p, k), zs.at[n]).wait()
    drain(0)
    drain(1)


def on_device(right_sides, pencil_s, pencil_t, value_alpha, value_beta, selected, block_slot, right_basis, vectors):
    zt = right_basis.transpose(1, 2, 0).reshape(64, ORD)
    vm = pl.BlockSpec(memory_space=pltpu.VMEM)
    dma = pltpu.SemaphoreType.DMA
    sides, prod = pl.pallas_call(
        kernel,
        out_shape=(jax.ShapeDtypeStruct((512, 128), F32), jax.ShapeDtypeStruct((ORD, 128), F32)),
        in_specs=[vm] * 4 + [pl.BlockSpec(memory_space=pltpu.HBM)] * 4,
        out_specs=(vm, vm),
        scratch_shapes=[
            pltpu.VMEM((512, 128), F32),
            pltpu.VMEM((512, 512), F32),
            pltpu.VMEM((512, 512), F32),
            pltpu.VMEM((8, 64, ORD), F32),
            pltpu.VMEM((ORD, 512), BF),
            pltpu.VMEM((ORD, 512), BF),
            pltpu.VMEM((BLK, BLK), F32),
            pltpu.VMEM((BLK, BLK), F32),
            pltpu.VMEM((2, 512, 256), BF),
            pltpu.VMEM((BLK, 128), F32),
            pltpu.VMEM((2, BLK, 128), F32),
            pltpu.VMEM((2, 8, SUB, 128), F32),
            pltpu.VMEM((2, 4, SUB, 128), F32),
            pltpu.VMEM((2, BLK, 128), F32),
            pltpu.VMEM((256, 128), F32),
            pltpu.VMEM((SUB, SUB, 128), F32),
            pltpu.VMEM((8, 128), F32),
            dma((8, NCH)), dma((7 * NCH,)),
            dma((2, 8)), dma((2, 8)), dma((2, 4)), dma((2, 4)), dma((2, 8)), dma((2, 8)),
            dma((4,)),
        ],
        compiler_params=pltpu.CompilerParams(
            collective_id=0, has_side_effects=True, vmem_limit_bytes=60 << 20
        ),
    )(
        block_slot.reshape(1, 64), value_alpha.reshape(32, 128), value_beta.reshape(32, 128),
        selected.reshape(1, 128), right_sides, pencil_s, pencil_t, zt,
    )
    return sides, vectors + prod


def solution(mesh):
    return jax.shard_map(
        on_device,
        mesh=mesh,
        in_specs=(
            P("row", "col"), P("row", None), P("row", None), P(), P(), P("col"), P(),
            P("row", None, "col"), P("row", "col"),
        ),
        out_specs=(P("row", "col"), P("row", "col")),
        check_vma=False,
    )
```

```python
import functools

import jax
import jax.numpy as jnp
from jax import lax
from jax.experimental import pallas as pl
from jax.experimental.pallas import tpu as pltpu
from jax.sharding import PartitionSpec as P

MESH = pl.DeviceIdType.MESH
BLK = 256
SUB = 32
PANELS = BLK // SUB
NCH = 8
ORD = 2048
CH = ORD // NCH
F32 = jnp.float32
BF = jnp.bfloat16
Z_A = 3


def split(v):
    hi = v.astype(BF)
    return hi, (v - hi.astype(F32)).astype(BF)


def dot(a, b):
    return jnp.dot(a, b, preferred_element_type=F32)


def kernel(
    slot_ref, alpha_ref, beta_ref, sel_ref, side_hbm, s_hbm, t_hbm, zt,
    out_side, out_vec,
    side_ref, s_ref, t_ref, zbuf, zhi, zlow, xcat, sd, td, lmat, rbuf, cand, st1, st2, xw, xpad, coef, shifts,
    zr, zs, s1r, s1s, s2r, s2s, s3r, s3s, lsem,
):
    row = lax.axis_index("row")
    col = lax.axis_index("col")
    zlo = row // 8
    pi = row % 8
    zh = col // 4
    y = col % 4
    yp, ym, y2 = (y + 1) % 4, (y + 3) % 4, (y + 2) % 4
    oh = 1 - zh

    loads = []
    for n, (src, dst) in enumerate(((s_hbm, s_ref), (t_hbm, t_ref), (side_hbm, side_ref), (zt, zbuf.at[col]))):
        loads.append(pltpu.make_async_copy(src, dst, lsem.at[n]))
        loads[-1].start()

    bar = pltpu.get_barrier_semaphore()
    peers = [(row, zh * 4 + yp), (row, zh * 4 + ym), (row, oh * 4 + y)]
    peers += [(zlo * 8 + (pi + d) % 8, col) for d in range(1, 8)]
    peers += [(((zlo + d) % 4) * 8 + pi, col) for d in range(1, 4)]
    for d in peers:
        pl.semaphore_signal(bar, inc=1, device_id=d, device_id_type=MESH)

    zsends = []

    def piece(p, k):
        return zbuf.at[p, :, pl.ds(k * CH, CH)]

    def zsend(src, p, k, dcol):
        n = len(zsends)
        c = pltpu.make_async_remote_copy(
            src_ref=src, dst_ref=piece(p, k), send_sem=zs.at[n], recv_sem=zr.at[p, k],
            device_id=(row, dcol), device_id_type=MESH,
        )
        c.start()
        zsends.append((p, k))

    def zwait(p, k):
        pltpu.make_async_copy(piece(p, k), piece(p, k), zr.at[p, k]).wait()

    def own(k):
        return zt.at[:, pl.ds(k * CH, CH)]

    cp, cm, c2 = zh * 4 + yp, zh * 4 + ym, zh * 4 + y2
    q, qp, qm, q2 = oh * 4 + y, oh * 4 + yp, oh * 4 + ym, oh * 4 + y2

    def send_z(ks):
        for k in ks:
            zsend(own(k), col, k, q)

    def send_own():
        for k in range(NCH):
            zsend(own(k), col, k, cp)
            zsend(own(k), col, k, cm)

    def forward_own(ks):
        for k in ks:
            if k % 2 == 0:
                zwait(cm, k)
                zsend(piece(cm, k), cm, k, cp)
            else:
                zwait(cp, k)
                zsend(piece(cp, k), cp, k, cm)

    def send_far(ks):
        for k in ks:
            zwait(q, k)
            zsend(piece(q, k), q, k, cp)
            zsend(piece(q, k), q, k, cm)

    def forward_far(ks):
        for k in ks:
            if k % 2 == 0:
                zwait(qm, k)
                zsend(piece(qm, k), qm, k, cp)
            else:
                zwait(qp, k)
                zsend(piece(qp, k), qp, k, cm)


    sel = sel_ref[...]
    hot = (lax.broadcasted_iota(jnp.int32, (128, 128), 0) == sel % 128).astype(F32)
    rows_hot = lax.broadcasted_iota(jnp.int32, (32, 128), 0) == sel // 128

    def lookup(table):
        got = jnp.dot(table, hot, precision=lax.Precision.HIGHEST, preferred_element_type=F32)
        return jnp.sum(jnp.where(rows_hot, got, 0.0), axis=0, keepdims=True)

    shifts[0:1] = lookup(alpha_ref[...])
    shifts[1:2] = lookup(beta_ref[...])
    alpha = shifts[0:1]
    beta = shifts[1:2]

    slots = [slot_ref[0:1, 63:64], slot_ref[0:1, 62:63]]

    def half(ref, w, lanes):
        odd = jnp.broadcast_to(slots[w] % 2 == 1, (BLK, lanes.stop - lanes.start))
        return jnp.where(odd, ref[BLK:, lanes], ref[:BLK, lanes])

    def pick(ref, w, which, count):
        got = ref[w, 0]
        for i in range(1, count):
            got = jnp.where(jnp.broadcast_to(which == i, (SUB, 128)), ref[w, i], got)
        return got

    def prepare(w):
        cols = slice(BLK, 2 * BLK) if w == 0 else slice(0, BLK)
        s_diag = half(s_ref, w, cols)
        t_diag = half(t_ref, w, cols)
        sd[...] = s_diag
        td[...] = t_diag
        s_hi, s_lo = split(s_diag)
        t_hi, t_lo = split(t_diag)
        for g in range(2):
            c = slice(g * 128, g * 128 + 128)
            lmat[g, 0:256, 0:128] = s_hi[:, c]
            lmat[g, 0:256, 128:256] = t_hi[:, c]
            lmat[g, 256:512, 0:128] = s_lo[:, c]
            lmat[g, 256:512, 128:256] = t_lo[:, c]
        rbuf[...] = half(side_ref, w, slice(0, 128))

    lane = lax.broadcasted_iota(jnp.int32, (SUB, 128), 1)
    subl = lax.broadcasted_iota(jnp.int32, (SUB, 128), 0)

    def coefficients(p, b):
        r0 = pl.multiple_of(p * SUB, SUB)
        lanes = pl.ds(pl.multiple_of((p // 4) * 128, 128), 128)
        turn = (128 - (p % 4) * SUB) % 128
        s_rows = pltpu.roll(sd[pl.ds(r0, SUB), lanes], turn, 1)
        t_rows = pltpu.roll(td[pl.ds(r0, SUB), lanes], turn, 1)
        on_diag = lane == subl
        s_d = jnp.sum(jnp.where(on_diag, s_rows, 0.0), axis=1, keepdims=True)
        t_d = jnp.sum(jnp.where(on_diag, t_rows, 0.0), axis=1, keepdims=True)
        inv = 1.0 / (beta * s_d - alpha * t_d)
        for j in range(1, SUB):
            h = 8 * (j // 8 + 1)
            c_j = beta * s_rows[0:h, j:j + 1] - alpha * t_rows[0:h, j:j + 1]
            coef[b, j, 0:h] = jnp.where(subl[0:h] < j, c_j * inv[j:j + 1], 0.0)
        coef[b, 0] = inv

    def solve(w, hooks):
        xpad[...] = jnp.zeros_like(xpad)

        def pair(t2, _):
            for b in range(2):
                t = 2 * t2 + b
                p = PANELS - 1 - t
                for at, hook in hooks.items():
                    if at % 2 == b:
                        pl.when(t2 == at // 2)(hook)
                r0 = pl.multiple_of(p * SUB, SUB)
                off = pl.multiple_of((p % 4) * SUB, SUB)
                r = [rbuf[pl.ds(r0 + 8 * i, 8), :] for i in range(4)]
                for j in reversed(range(1, SUB)):
                    i = j // 8
                    entry = jnp.broadcast_to(r[i][j % 8:j % 8 + 1], (8, 128))
                    for a in range(i + 1):
                        r[a] = r[a] - coef[b, j, 8 * a:8 * a + 8] * entry
                x_p = jnp.concatenate(r, 0) * coef[b, 0]
                cand[w, pl.ds(r0, SUB)] = x_p

                @pl.when(p != pi)
                def _():
                    stage1(w, p).start()

                @pl.when(p == pi)
                def _():
                    st1[w, pi] = cand[w, pl.ds(r0, SUB)]

                xpad[pl.ds(off, SUB)] = beta * x_p
                xpad[pl.ds(128 + off, SUB)] = -(alpha * x_p)
                hi, lo = split(xpad[...])
                prod = dot(lmat[p // 4], jnp.concatenate([hi, lo], 1))
                coefficients(lax.rem(p + PANELS - 1, PANELS), 1 - b)
                rbuf[...] -= prod[0:256, 0:128] + (prod[0:256, 128:256] + prod[256:512, 0:128])
                xpad[pl.ds(off, SUB)] = jnp.zeros((SUB, 128), F32)
                xpad[pl.ds(128 + off, SUB)] = jnp.zeros((SUB, 128), F32)
            return 0

        lax.fori_loop(0, PANELS // 2, pair, 0)

    def stage1(w, p):
        return pltpu.make_async_remote_copy(
            src_ref=cand.at[w, pl.ds(pl.multiple_of(p * SUB, SUB), SUB)], dst_ref=st1.at[w, pi],
            send_sem=s1s.at[w, p], recv_sem=s1r.at[w, pi],
            device_id=(zlo * 8 + p, col), device_id_type=MESH,
        )

    def stage2(w):
        owner = slots[w] // 2
        for d in range(1, 8):
            src = (pi + d) % 8
            pltpu.make_async_copy(st1.at[w, src], st1.at[w, src], s1r.at[w, src]).wait()
        st2[w, zlo] = pick(st1, w, owner % 8, 8)
        for d in range(1, 4):
            pltpu.make_async_remote_copy(
                src_ref=st2.at[w, zlo], dst_ref=st2.at[w, zlo],
                send_sem=s2s.at[w, d], recv_sem=s2r.at[w, zlo],
                device_id=(((zlo + d) % 4) * 8 + pi, col), device_id_type=MESH,
            ).start()

    def mine():
        return pl.ds(pl.multiple_of(pi * SUB, SUB), SUB)

    def stage3(w):
        owner = slots[w] // 2
        for d in range(1, 4):
            src = (zlo + d) % 4
            pltpu.make_async_copy(st2.at[w, src], st2.at[w, src], s2r.at[w, src]).wait()
        xw[w, mine()] = pick(st2, w, owner // 8, 4)
        for d in range(1, 8):
            pltpu.make_async_remote_copy(
                src_ref=xw.at[w, mine()], dst_ref=xw.at[w, mine()],
                send_sem=s3s.at[w, d], recv_sem=s3r.at[w, pi],
                device_id=(zlo * 8 + (pi + d) % 8, col), device_id_type=MESH,
            ).start()

    def stage4(w):
        for d in range(1, 8):
            src = (pi + d) % 8
            part = xw.at[w, pl.ds(pl.multiple_of(src * SUB, SUB), SUB)]
            pltpu.make_async_copy(part, part, s3r.at[w, src]).wait()

    def drain(w):
        for d in range(1, 8):
            p = (pi + d) % 8
            stage1(w, p).wait_send()
            pltpu.make_async_copy(xw.at[w, mine()], xw.at[w, mine()], s3s.at[w, d]).wait()
        for d in range(1, 4):
            pltpu.make_async_copy(st2.at[w, zlo], st2.at[w, zlo], s2s.at[w, d]).wait()

    def apply(s_cols, t_cols, x):
        lh, ll = split(jnp.concatenate([s_cols, t_cols], 1))
        rh, rl = split(jnp.concatenate([beta * x, -(alpha * x)], 0))
        wide = dot(lh, jnp.concatenate([rh, rl], 1))
        return wide[:, 0:128] + (wide[:, 128:256] + dot(ll, rh))

    order = [col, cp, cm, c2, q, qp, qm, q2]

    def convert(pair, m):
        first, second = order[2 * pair], order[2 * pair + 1]
        rows = pl.ds(m * CH, CH)
        both = jnp.concatenate([zbuf[first, :, rows], zbuf[second, :, rows]], 0)
        hi, lo = split(both.T)
        zhi[rows, 128 * pair:128 * pair + 128] = hi
        zlow[rows, 128 * pair:128 * pair + 128] = lo

    def convert_all(pair):
        def chunk(m, _):
            convert(pair, m)
            return 0

        lax.fori_loop(0, NCH, chunk, 0)

    def gather_x():
        for n, c in enumerate(order):
            at = pl.ds(pl.multiple_of(c * SUB, SUB), SUB)
            for h in range(2):
                hi, lo = split(xw[1 - h, at])
                rows = slice(64 * n + SUB * h, 64 * n + SUB * h + SUB)
                xcat[rows, 0:128] = hi
                xcat[rows, 128:256] = lo

    def product(m):
        rows = pl.ds(m * CH, CH)
        wide = dot(zhi[rows, :], xcat[...])
        out_vec[rows, :] = wide[:, 0:128] + (wide[:, 128:256] + dot(zlow[rows, :], xcat[:, 0:128]))

    right = slice(BLK, 2 * BLK)
    for c in loads[:3]:
        c.wait()
    prepare(0)
    coefficients(PANELS - 1, 0)
    pl.semaphore_wait(bar, len(peers))
    send_z(range(Z_A))
    send_own()
    solve(0, {})
    stage2(0)
    forward_own(range(0, 4))
    prepare(1)
    coefficients(PANELS - 1, 0)
    stage3(0)
    send_z(range(Z_A, NCH))
    forward_own(range(4, NCH))
    send_far(range(Z_A))
    stage4(0)
    rbuf[...] -= apply(half(s_ref, 1, right), half(t_ref, 1, right), xw[0])
    solve(1, {})
    stage2(1)
    send_far(range(Z_A, Z_A + 2))
    for h in range(2):
        rs = slice(h * BLK, h * BLK + BLK)
        out_side[rs, :] = side_ref[rs, :] - apply(s_ref[rs, BLK:], t_ref[rs, BLK:], xw[0])
    loads[3].wait()
    for k in range(NCH):
        zwait(cp if k % 2 == 0 else cm, k)
    convert_all(0)
    forward_far(range(0, 2))
    send_far(range(Z_A + 2, Z_A + 3))
    for k in range(NCH):
        zwait(c2, k)
    convert_all(1)
    forward_far(range(2, 3))
    stage3(1)
    send_far(range(Z_A + 3, NCH))
    forward_far(range(3, 5))
    stage4(1)
    gather_x()
    for h in range(2):
        rs = slice(h * BLK, h * BLK + BLK)
        new = out_side[rs, :] - apply(s_ref[rs, :BLK], t_ref[rs, :BLK], xw[1])
        here = row * 2 + h
        new = jnp.where(jnp.broadcast_to(slots[1] == here, (BLK, 128)), xw[1], new)
        out_side[rs, :] = jnp.where(jnp.broadcast_to(slots[0] == here, (BLK, 128)), xw[0], new)

    for k in range(NCH):
        if 5 <= k + 4 < NCH:
            forward_far([k + 4])
        zwait(qp if k % 2 == 0 else qm, k)
        zwait(q2, k)
        convert(2, k)
        convert(3, k)
        product(k)
    for n, (p, k) in enumerate(zsends):
        pltpu.make_async_copy(piece(p, k), piece(p, k), zs.at[n]).wait()
    drain(0)
    drain(1)


def on_device(right_sides, pencil_s, pencil_t, value_alpha, value_beta, selected, block_slot, right_basis, vectors):
    zt = right_basis.transpose(1, 2, 0).reshape(64, ORD)
    vm = pl.BlockSpec(memory_space=pltpu.VMEM)
    dma = pltpu.SemaphoreType.DMA
    sides, prod = pl.pallas_call(
        kernel,
        out_shape=(jax.ShapeDtypeStruct((512, 128), F32), jax.ShapeDtypeStruct((ORD, 128), F32)),
        in_specs=[vm] * 4 + [pl.BlockSpec(memory_space=pltpu.HBM)] * 4,
        out_specs=(vm, vm),
        scratch_shapes=[
            pltpu.VMEM((512, 128), F32),
            pltpu.VMEM((512, 512), F32),
            pltpu.VMEM((512, 512), F32),
            pltpu.VMEM((8, 64, ORD), F32),
            pltpu.VMEM((ORD, 512), BF),
            pltpu.VMEM((ORD, 512), BF),
            pltpu.VMEM((512, 256), BF),
            pltpu.VMEM((BLK, BLK), F32),
            pltpu.VMEM((BLK, BLK), F32),
            pltpu.VMEM((2, 512, 256), BF),
            pltpu.VMEM((BLK, 128), F32),
            pltpu.VMEM((2, BLK, 128), F32),
            pltpu.VMEM((2, 8, SUB, 128), F32),
            pltpu.VMEM((2, 4, SUB, 128), F32),
            pltpu.VMEM((2, BLK, 128), F32),
            pltpu.VMEM((256, 128), F32),
            pltpu.VMEM((2, SUB, SUB, 128), F32),
            pltpu.VMEM((8, 128), F32),
            dma((8, NCH)), dma((7 * NCH,)),
            dma((2, 8)), dma((2, 8)), dma((2, 4)), dma((2, 4)), dma((2, 8)), dma((2, 8)),
            dma((4,)),
        ],
        compiler_params=pltpu.CompilerParams(
            collective_id=0, has_side_effects=True, vmem_limit_bytes=48 << 20
        ),
    )(
        *(pltpu.with_memory_space_constraint(v, pltpu.HBM) for v in (
            block_slot.reshape(1, 64), value_alpha.reshape(32, 128), value_beta.reshape(32, 128),
            selected.reshape(1, 128), right_sides, pencil_s, pencil_t, zt,
        )),
    )
    return sides, vectors + prod


def solution(mesh):
    return jax.shard_map(
        on_device,
        mesh=mesh,
        in_specs=(
            P("row", "col"), P("row", None), P("row", None), P(), P(), P("col"), P(),
            P("row", None, "col"), P("row", "col"),
        ),
        out_specs=(P("row", "col"), P("row", "col")),
        check_vma=False,
    )
```

```python
import functools

import jax
import jax.numpy as jnp
from jax import lax
from jax.experimental import pallas as pl
from jax.experimental.pallas import tpu as pltpu
from jax.sharding import PartitionSpec as P

MESH = pl.DeviceIdType.MESH
BLK = 256
SUB = 32
PANELS = BLK // SUB
NCH = 8
ORD = 2048
CH = ORD // NCH
F32 = jnp.float32
BF = jnp.bfloat16
Z_A = 3


def split(v):
    hi = v.astype(BF)
    return hi, (v - hi.astype(F32)).astype(BF)


def dot(a, b):
    return jnp.dot(a, b, preferred_element_type=F32)


def kernel(
    slot_hbm, alpha_hbm, beta_hbm, sel_hbm, side_hbm, s_hbm, t_hbm, zt,
    out_side, out_vec,
    slot_ref, alpha_ref, beta_ref, sel_ref, side_ref, s_ref, t_ref, zbuf, zhi, zlow, xcat, sd, td, lmat, rbuf, cand, st1, st2, xw, xpad, coef, shifts,
    zr, zs, s1r, s1s, s2r, s2s, s3r, s3s, lsem,
):
    row = lax.axis_index("row")
    col = lax.axis_index("col")
    zlo = row // 8
    pi = row % 8
    zh = col // 4
    y = col % 4
    yp, ym, y2 = (y + 1) % 4, (y + 3) % 4, (y + 2) % 4
    oh = 1 - zh

    bar = pltpu.get_barrier_semaphore()
    peers = [(row, zh * 4 + yp), (row, zh * 4 + ym), (row, oh * 4 + y)]
    peers += [(zlo * 8 + (pi + d) % 8, col) for d in range(1, 8)]
    peers += [(((zlo + d) % 4) * 8 + pi, col) for d in range(1, 4)]
    for d in peers:
        pl.semaphore_signal(bar, inc=1, device_id=d, device_id_type=MESH)

    loads = []
    for n, (src, dst) in enumerate((
        (slot_hbm, slot_ref), (alpha_hbm, alpha_ref), (beta_hbm, beta_ref), (sel_hbm, sel_ref),
        (s_hbm, s_ref), (t_hbm, t_ref), (side_hbm, side_ref), (zt, zbuf.at[col]),
    )):
        loads.append(pltpu.make_async_copy(src, dst, lsem.at[n]))
        loads[-1].start()

    zsends = []

    def piece(p, k):
        return zbuf.at[p, :, pl.ds(k * CH, CH)]

    def zsend(src, p, k, dcol):
        n = len(zsends)
        c = pltpu.make_async_remote_copy(
            src_ref=src, dst_ref=piece(p, k), send_sem=zs.at[n], recv_sem=zr.at[p, k],
            device_id=(row, dcol), device_id_type=MESH,
        )
        c.start()
        zsends.append((p, k))

    def zwait(p, k):
        pltpu.make_async_copy(piece(p, k), piece(p, k), zr.at[p, k]).wait()

    def own(k):
        return zt.at[:, pl.ds(k * CH, CH)]

    cp, cm, c2 = zh * 4 + yp, zh * 4 + ym, zh * 4 + y2
    q, qp, qm, q2 = oh * 4 + y, oh * 4 + yp, oh * 4 + ym, oh * 4 + y2

    def send_z(ks):
        for k in ks:
            zsend(own(k), col, k, q)

    def send_own():
        for k in range(NCH):
            zsend(own(k), col, k, cp)
            zsend(own(k), col, k, cm)

    def forward_own(ks):
        for k in ks:
            if k % 2 == 0:
                zwait(cm, k)
                zsend(piece(cm, k), cm, k, cp)
            else:
                zwait(cp, k)
                zsend(piece(cp, k), cp, k, cm)

    def send_far(ks):
        for k in ks:
            zwait(q, k)
            zsend(piece(q, k), q, k, cp)
            zsend(piece(q, k), q, k, cm)

    def forward_far(ks):
        for k in ks:
            if k % 2 == 0:
                zwait(qm, k)
                zsend(piece(qm, k), qm, k, cp)
            else:
                zwait(qp, k)
                zsend(piece(qp, k), qp, k, cm)


    for c in loads[:4]:
        c.wait()
    sel = sel_ref[...]
    hot = (lax.broadcasted_iota(jnp.int32, (128, 128), 0) == sel % 128).astype(F32)
    rows_hot = lax.broadcasted_iota(jnp.int32, (32, 128), 0) == sel // 128

    def lookup(table):
        got = jnp.dot(table, hot, precision=lax.Precision.HIGHEST, preferred_element_type=F32)
        return jnp.sum(jnp.where(rows_hot, got, 0.0), axis=0, keepdims=True)

    shifts[0:1] = lookup(alpha_ref[...])
    shifts[1:2] = lookup(beta_ref[...])
    alpha = shifts[0:1]
    beta = shifts[1:2]

    slots = [slot_ref[0:1, 63:64], slot_ref[0:1, 62:63]]

    def half(ref, w, lanes):
        odd = jnp.broadcast_to(slots[w] % 2 == 1, (BLK, lanes.stop - lanes.start))
        return jnp.where(odd, ref[BLK:, lanes], ref[:BLK, lanes])

    def pick(ref, w, which, count):
        got = ref[w, 0]
        for i in range(1, count):
            got = jnp.where(jnp.broadcast_to(which == i, (SUB, 128)), ref[w, i], got)
        return got

    def prepare(w):
        cols = slice(BLK, 2 * BLK) if w == 0 else slice(0, BLK)
        s_diag = half(s_ref, w, cols)
        t_diag = half(t_ref, w, cols)
        sd[...] = s_diag
        td[...] = t_diag
        s_hi, s_lo = split(s_diag)
        t_hi, t_lo = split(t_diag)
        for g in range(2):
            c = slice(g * 128, g * 128 + 128)
            lmat[g, 0:256, 0:128] = s_hi[:, c]
            lmat[g, 0:256, 128:256] = t_hi[:, c]
            lmat[g, 256:512, 0:128] = s_lo[:, c]
            lmat[g, 256:512, 128:256] = t_lo[:, c]
        rbuf[...] = half(side_ref, w, slice(0, 128))

    lane = lax.broadcasted_iota(jnp.int32, (SUB, 128), 1)
    subl = lax.broadcasted_iota(jnp.int32, (SUB, 128), 0)

    def coefficients(p, b):
        r0 = pl.multiple_of(p * SUB, SUB)
        lanes = pl.ds(pl.multiple_of((p // 4) * 128, 128), 128)
        turn = (128 - (p % 4) * SUB) % 128
        s_rows = pltpu.roll(sd[pl.ds(r0, SUB), lanes], turn, 1)
        t_rows = pltpu.roll(td[pl.ds(r0, SUB), lanes], turn, 1)
        on_diag = lane == subl
        s_d = jnp.sum(jnp.where(on_diag, s_rows, 0.0), axis=1, keepdims=True)
        t_d = jnp.sum(jnp.where(on_diag, t_rows, 0.0), axis=1, keepdims=True)
        inv = 1.0 / (beta * s_d - alpha * t_d)
        for j in range(1, SUB):
            h = 8 * (j // 8 + 1)
            c_j = beta * s_rows[0:h, j:j + 1] - alpha * t_rows[0:h, j:j + 1]
            coef[b, j, 0:h] = jnp.where(subl[0:h] < j, c_j * inv[j:j + 1], 0.0)
        coef[b, 0] = inv

    def solve(w, hooks):
        xpad[...] = jnp.zeros_like(xpad)

        def pair(t2, _):
            for b in range(2):
                t = 2 * t2 + b
                p = PANELS - 1 - t
                for at, hook in hooks.items():
                    if at % 2 == b:
                        pl.when(t2 == at // 2)(hook)
                r0 = pl.multiple_of(p * SUB, SUB)
                off = pl.multiple_of((p % 4) * SUB, SUB)
                r = [rbuf[pl.ds(r0 + 8 * i, 8), :] for i in range(4)]
                for j in reversed(range(1, SUB)):
                    i = j // 8
                    entry = jnp.broadcast_to(r[i][j % 8:j % 8 + 1], (8, 128))
                    for a in range(i + 1):
                        r[a] = r[a] - coef[b, j, 8 * a:8 * a + 8] * entry
                x_p = jnp.concatenate(r, 0) * coef[b, 0]
                cand[w, pl.ds(r0, SUB)] = x_p

                @pl.when(p != pi)
                def _():
                    stage1(w, p).start()

                @pl.when(p == pi)
                def _():
                    st1[w, pi] = cand[w, pl.ds(r0, SUB)]

                xpad[pl.ds(off, SUB)] = beta * x_p
                xpad[pl.ds(128 + off, SUB)] = -(alpha * x_p)
                hi, lo = split(xpad[...])
                prod = dot(lmat[p // 4], jnp.concatenate([hi, lo], 1))
                coefficients(lax.rem(p + PANELS - 1, PANELS), 1 - b)
                rbuf[...] -= prod[0:256, 0:128] + (prod[0:256, 128:256] + prod[256:512, 0:128])
                xpad[pl.ds(off, SUB)] = jnp.zeros((SUB, 128), F32)
                xpad[pl.ds(128 + off, SUB)] = jnp.zeros((SUB, 128), F32)
            return 0

        lax.fori_loop(0, PANELS // 2, pair, 0)

    def stage1(w, p):
        return pltpu.make_async_remote_copy(
            src_ref=cand.at[w, pl.ds(pl.multiple_of(p * SUB, SUB), SUB)], dst_ref=st1.at[w, pi],
            send_sem=s1s.at[w, p], recv_sem=s1r.at[w, pi],
            device_id=(zlo * 8 + p, col), device_id_type=MESH,
        )

    def stage2(w):
        owner = slots[w] // 2
        for d in range(1, 8):
            src = (pi + d) % 8
            pltpu.make_async_copy(st1.at[w, src], st1.at[w, src], s1r.at[w, src]).wait()
        st2[w, zlo] = pick(st1, w, owner % 8, 8)
        for d in range(1, 4):
            pltpu.make_async_remote_copy(
                src_ref=st2.at[w, zlo], dst_ref=st2.at[w, zlo],
                send_sem=s2s.at[w, d], recv_sem=s2r.at[w, zlo],
                device_id=(((zlo + d) % 4) * 8 + pi, col), device_id_type=MESH,
            ).start()

    def mine():
        return pl.ds(pl.multiple_of(pi * SUB, SUB), SUB)

    def stage3(w):
        owner = slots[w] // 2
        for d in range(1, 4):
            src = (zlo + d) % 4
            pltpu.make_async_copy(st2.at[w, src], st2.at[w, src], s2r.at[w, src]).wait()
        xw[w, mine()] = pick(st2, w, owner // 8, 4)
        for d in range(1, 8):
            pltpu.make_async_remote_copy(
                src_ref=xw.at[w, mine()], dst_ref=xw.at[w, mine()],
                send_sem=s3s.at[w, d], recv_sem=s3r.at[w, pi],
                device_id=(zlo * 8 + (pi + d) % 8, col), device_id_type=MESH,
            ).start()

    def stage4(w):
        for d in range(1, 8):
            src = (pi + d) % 8
            part = xw.at[w, pl.ds(pl.multiple_of(src * SUB, SUB), SUB)]
            pltpu.make_async_copy(part, part, s3r.at[w, src]).wait()

    def drain(w):
        for d in range(1, 8):
            p = (pi + d) % 8
            stage1(w, p).wait_send()
            pltpu.make_async_copy(xw.at[w, mine()], xw.at[w, mine()], s3s.at[w, d]).wait()
        for d in range(1, 4):
            pltpu.make_async_copy(st2.at[w, zlo], st2.at[w, zlo], s2s.at[w, d]).wait()

    def apply(s_cols, t_cols, x):
        lh, ll = split(jnp.concatenate([s_cols, t_cols], 1))
        rh, rl = split(jnp.concatenate([beta * x, -(alpha * x)], 0))
        wide = dot(lh, jnp.concatenate([rh, rl], 1))
        return wide[:, 0:128] + (wide[:, 128:256] + dot(ll, rh))

    order = [col, cp, cm, c2, q, qp, qm, q2]

    def convert(pair, m):
        first, second = order[2 * pair], order[2 * pair + 1]
        rows = pl.ds(m * CH, CH)
        both = jnp.concatenate([zbuf[first, :, rows], zbuf[second, :, rows]], 0)
        hi, lo = split(both.T)
        zhi[rows, 128 * pair:128 * pair + 128] = hi
        zlow[rows, 128 * pair:128 * pair + 128] = lo

    def convert_all(pair):
        def chunk(m, _):
            convert(pair, m)
            return 0

        lax.fori_loop(0, NCH, chunk, 0)

    def gather_x():
        for n, c in enumerate(order):
            at = pl.ds(pl.multiple_of(c * SUB, SUB), SUB)
            for h in range(2):
                hi, lo = split(xw[1 - h, at])
                rows = slice(64 * n + SUB * h, 64 * n + SUB * h + SUB)
                xcat[rows, 0:128] = hi
                xcat[rows, 128:256] = lo

    def product(m):
        rows = pl.ds(m * CH, CH)
        wide = dot(zhi[rows, :], xcat[...])
        out_vec[rows, :] = wide[:, 0:128] + (wide[:, 128:256] + dot(zlow[rows, :], xcat[:, 0:128]))

    right = slice(BLK, 2 * BLK)
    for c in loads[4:7]:
        c.wait()
    pl.semaphore_wait(bar, len(peers))
    send_z(range(Z_A))
    send_own()
    prepare(0)
    coefficients(PANELS - 1, 0)
    solve(0, {})
    stage2(0)
    forward_own(range(0, 4))
    prepare(1)
    coefficients(PANELS - 1, 0)
    stage3(0)
    send_z(range(Z_A, NCH))
    forward_own(range(4, NCH))
    send_far(range(Z_A))
    stage4(0)
    rbuf[...] -= apply(half(s_ref, 1, right), half(t_ref, 1, right), xw[0])
    solve(1, {})
    stage2(1)
    send_far(range(Z_A, Z_A + 2))
    for h in range(2):
        rs = slice(h * BLK, h * BLK + BLK)
        out_side[rs, :] = side_ref[rs, :] - apply(s_ref[rs, BLK:], t_ref[rs, BLK:], xw[0])
    loads[7].wait()
    for k in range(NCH):
        zwait(cp if k % 2 == 0 else cm, k)
    convert_all(0)
    forward_far(range(0, 2))
    send_far(range(Z_A + 2, Z_A + 3))
    for k in range(NCH):
        zwait(c2, k)
    convert_all(1)
    forward_far(range(2, 3))
    stage3(1)
    send_far(range(Z_A + 3, NCH))
    forward_far(range(3, 8))
    early = 2
    for k in range(early):
        zwait(qp if k % 2 == 0 else qm, k)
        zwait(q2, k)
        convert(2, k)
        convert(3, k)
    stage4(1)
    gather_x()
    for h in range(2):
        rs = slice(h * BLK, h * BLK + BLK)
        new = out_side[rs, :] - apply(s_ref[rs, :BLK], t_ref[rs, :BLK], xw[1])
        here = row * 2 + h
        new = jnp.where(jnp.broadcast_to(slots[1] == here, (BLK, 128)), xw[1], new)
        out_side[rs, :] = jnp.where(jnp.broadcast_to(slots[0] == here, (BLK, 128)), xw[0], new)

    for k in range(NCH):
        if k >= early:
            zwait(qp if k % 2 == 0 else qm, k)
            zwait(q2, k)
            convert(2, k)
            convert(3, k)
        product(k)
    for n, (p, k) in enumerate(zsends):
        pltpu.make_async_copy(piece(p, k), piece(p, k), zs.at[n]).wait()
    drain(0)
    drain(1)


def on_device(right_sides, pencil_s, pencil_t, value_alpha, value_beta, selected, block_slot, right_basis, vectors):
    zt = right_basis.transpose(1, 2, 0).reshape(64, ORD)
    vm = pl.BlockSpec(memory_space=pltpu.VMEM)
    dma = pltpu.SemaphoreType.DMA
    sides, prod = pl.pallas_call(
        kernel,
        out_shape=(jax.ShapeDtypeStruct((512, 128), F32), jax.ShapeDtypeStruct((ORD, 128), F32)),
        in_specs=[pl.BlockSpec(memory_space=pltpu.HBM)] * 8,
        out_specs=(vm, vm),
        scratch_shapes=[
            pltpu.VMEM((1, 64), jnp.int32),
            pltpu.VMEM((32, 128), F32),
            pltpu.VMEM((32, 128), F32),
            pltpu.VMEM((1, 128), jnp.int32),
            pltpu.VMEM((512, 128), F32),
            pltpu.VMEM((512, 512), F32),
            pltpu.VMEM((512, 512), F32),
            pltpu.VMEM((8, 64, ORD), F32),
            pltpu.VMEM((ORD, 512), BF),
            pltpu.VMEM((ORD, 512), BF),
            pltpu.VMEM((512, 256), BF),
            pltpu.VMEM((BLK, BLK), F32),
            pltpu.VMEM((BLK, BLK), F32),
            pltpu.VMEM((2, 512, 256), BF),
            pltpu.VMEM((BLK, 128), F32),
            pltpu.VMEM((2, BLK, 128), F32),
            pltpu.VMEM((2, 8, SUB, 128), F32),
            pltpu.VMEM((2, 4, SUB, 128), F32),
            pltpu.VMEM((2, BLK, 128), F32),
            pltpu.VMEM((256, 128), F32),
            pltpu.VMEM((2, SUB, SUB, 128), F32),
            pltpu.VMEM((8, 128), F32),
            dma((8, NCH)), dma((7 * NCH,)),
            dma((2, 8)), dma((2, 8)), dma((2, 4)), dma((2, 4)), dma((2, 8)), dma((2, 8)),
            dma((8,)),
        ],
        compiler_params=pltpu.CompilerParams(
            collective_id=0, has_side_effects=True, vmem_limit_bytes=48 << 20
        ),
    )(
        *(pltpu.with_memory_space_constraint(v, pltpu.HBM) for v in (
            block_slot.reshape(1, 64), value_alpha.reshape(32, 128), value_beta.reshape(32, 128),
            selected.reshape(1, 128), right_sides, pencil_s, pencil_t, zt,
        )),
    )
    return sides, vectors + prod


def solution(mesh):
    return jax.shard_map(
        on_device,
        mesh=mesh,
        in_specs=(
            P("row", "col"), P("row", None), P("row", None), P(), P(), P("col"), P(),
            P("row", None, "col"), P("row", "col"),
        ),
        out_specs=(P("row", "col"), P("row", "col")),
        check_vma=False,
    )
```

```python
import functools

import jax
import jax.numpy as jnp
from jax import lax
from jax.experimental import pallas as pl
from jax.experimental.pallas import tpu as pltpu
from jax.sharding import PartitionSpec as P

MESH = pl.DeviceIdType.MESH
BLK = 256
SUB = 32
PANELS = BLK // SUB
NCH = 8
ORD = 2048
CH = ORD // NCH
F32 = jnp.float32
BF = jnp.bfloat16
Z_A = 3


def split(v):
    hi = v.astype(BF)
    return hi, (v - hi.astype(F32)).astype(BF)


def dot(a, b):
    return jnp.dot(a, b, preferred_element_type=F32)


def kernel(
    slot_hbm, alpha_hbm, beta_hbm, sel_hbm, side_hbm, s_hbm, t_hbm, zt,
    out_side, out_vec,
    slot_ref, alpha_ref, beta_ref, sel_ref, side_ref, s_ref, t_ref, zbuf, zhi, zlow, xcat, sd, td, lmat, rbuf, cand, st1, st2, xw, xpad, coef, shifts,
    zr, zs, s1r, s1s, s2r, s2s, s3r, s3s, lsem,
):
    row = lax.axis_index("row")
    col = lax.axis_index("col")
    zlo = row // 8
    pi = row % 8
    zh = col // 4
    y = col % 4
    yp, ym, y2 = (y + 1) % 4, (y + 3) % 4, (y + 2) % 4
    oh = 1 - zh

    bar = pltpu.get_barrier_semaphore()
    peers = [(row, zh * 4 + yp), (row, zh * 4 + ym), (row, oh * 4 + y)]
    peers += [(zlo * 8 + (pi + d) % 8, col) for d in range(1, 8)]
    peers += [(((zlo + d) % 4) * 8 + pi, col) for d in range(1, 4)]
    for d in peers:
        pl.semaphore_signal(bar, inc=1, device_id=d, device_id_type=MESH)

    loads = []
    for n, (src, dst) in enumerate((
        (slot_hbm, slot_ref), (alpha_hbm, alpha_ref), (beta_hbm, beta_ref), (sel_hbm, sel_ref),
        (s_hbm, s_ref), (t_hbm, t_ref), (side_hbm, side_ref), (zt, zbuf.at[col]),
    )):
        loads.append(pltpu.make_async_copy(src, dst, lsem.at[n]))
        loads[-1].start()

    zsends = []

    def piece(p, k):
        return zbuf.at[p, :, pl.ds(k * CH, CH)]

    def zsend(src, p, k, dcol):
        n = len(zsends)
        c = pltpu.make_async_remote_copy(
            src_ref=src, dst_ref=piece(p, k), send_sem=zs.at[n], recv_sem=zr.at[p, k],
            device_id=(row, dcol), device_id_type=MESH,
        )
        c.start()
        zsends.append((p, k))

    def zwait(p, k):
        pltpu.make_async_copy(piece(p, k), piece(p, k), zr.at[p, k]).wait()

    def own(k):
        return zt.at[:, pl.ds(k * CH, CH)]

    cp, cm, c2 = zh * 4 + yp, zh * 4 + ym, zh * 4 + y2
    q, qp, qm, q2 = oh * 4 + y, oh * 4 + yp, oh * 4 + ym, oh * 4 + y2

    def send_z(ks):
        for k in ks:
            zsend(own(k), col, k, q)

    def send_own():
        for k in range(NCH):
            zsend(own(k), col, k, cp)
            zsend(own(k), col, k, cm)

    def forward_own(ks):
        for k in ks:
            if k % 2 == 0:
                zwait(cm, k)
                zsend(piece(cm, k), cm, k, cp)
            else:
                zwait(cp, k)
                zsend(piece(cp, k), cp, k, cm)

    def send_far(ks):
        for k in ks:
            zwait(q, k)
            zsend(piece(q, k), q, k, cp)
            zsend(piece(q, k), q, k, cm)

    def forward_far(ks):
        for k in ks:
            if k % 2 == 0:
                zwait(qm, k)
                zsend(piece(qm, k), qm, k, cp)
            else:
                zwait(qp, k)
                zsend(piece(qp, k), qp, k, cm)


    for c in loads[:4]:
        c.wait()
    sel = sel_ref[...]
    hot = (lax.broadcasted_iota(jnp.int32, (128, 128), 0) == sel % 128).astype(F32)
    rows_hot = lax.broadcasted_iota(jnp.int32, (32, 128), 0) == sel // 128

    def lookup(table):
        got = jnp.dot(table, hot, precision=lax.Precision.HIGHEST, preferred_element_type=F32)
        return jnp.sum(jnp.where(rows_hot, got, 0.0), axis=0, keepdims=True)

    shifts[0:1] = lookup(alpha_ref[...])
    shifts[1:2] = lookup(beta_ref[...])
    alpha = shifts[0:1]
    beta = shifts[1:2]

    slots = [slot_ref[0:1, 63:64], slot_ref[0:1, 62:63]]

    def half(ref, w, lanes):
        odd = jnp.broadcast_to(slots[w] % 2 == 1, (BLK, lanes.stop - lanes.start))
        return jnp.where(odd, ref[BLK:, lanes], ref[:BLK, lanes])

    def pick(ref, w, which, count):
        got = ref[w, 0]
        for i in range(1, count):
            got = jnp.where(jnp.broadcast_to(which == i, (SUB, 128)), ref[w, i], got)
        return got

    def prepare(w):
        cols = slice(BLK, 2 * BLK) if w == 0 else slice(0, BLK)
        s_diag = half(s_ref, w, cols)
        t_diag = half(t_ref, w, cols)
        sd[...] = s_diag
        td[...] = t_diag
        s_hi, s_lo = split(s_diag)
        t_hi, t_lo = split(t_diag)
        for g in range(2):
            c = slice(g * 128, g * 128 + 128)
            lmat[g, 0:256, 0:128] = s_hi[:, c]
            lmat[g, 0:256, 128:256] = t_hi[:, c]
            lmat[g, 256:512, 0:128] = s_lo[:, c]
            lmat[g, 256:512, 128:256] = t_lo[:, c]
        rbuf[...] = half(side_ref, w, slice(0, 128))

    lane = lax.broadcasted_iota(jnp.int32, (SUB, 128), 1)
    subl = lax.broadcasted_iota(jnp.int32, (SUB, 128), 0)

    def coefficients(p, b):
        r0 = pl.multiple_of(p * SUB, SUB)
        lanes = pl.ds(pl.multiple_of((p // 4) * 128, 128), 128)
        turn = (128 - (p % 4) * SUB) % 128
        s_rows = pltpu.roll(sd[pl.ds(r0, SUB), lanes], turn, 1)
        t_rows = pltpu.roll(td[pl.ds(r0, SUB), lanes], turn, 1)
        on_diag = lane == subl
        s_d = jnp.sum(jnp.where(on_diag, s_rows, 0.0), axis=1, keepdims=True)
        t_d = jnp.sum(jnp.where(on_diag, t_rows, 0.0), axis=1, keepdims=True)
        inv = 1.0 / (beta * s_d - alpha * t_d)
        for j in range(1, SUB):
            h = 8 * (j // 8 + 1)
            c_j = beta * s_rows[0:h, j:j + 1] - alpha * t_rows[0:h, j:j + 1]
            coef[b, j, 0:h] = jnp.where(subl[0:h] < j, c_j * inv[j:j + 1], 0.0)
        coef[b, 0] = inv

    def solve(w, hooks):
        xpad[...] = jnp.zeros_like(xpad)

        def pair(t2, _):
            for b in range(2):
                t = 2 * t2 + b
                p = PANELS - 1 - t
                for at, hook in hooks.items():
                    if at % 2 == b:
                        pl.when(t2 == at // 2)(hook)
                r0 = pl.multiple_of(p * SUB, SUB)
                off = pl.multiple_of((p % 4) * SUB, SUB)
                r = [rbuf[pl.ds(r0 + 8 * i, 8), :] for i in range(4)]
                for j in reversed(range(1, SUB)):
                    i = j // 8
                    entry = jnp.broadcast_to(r[i][j % 8:j % 8 + 1], (8, 128))
                    for a in range(i + 1):
                        r[a] = r[a] - coef[b, j, 8 * a:8 * a + 8] * entry
                x_p = jnp.concatenate(r, 0) * coef[b, 0]
                cand[w, pl.ds(r0, SUB)] = x_p

                @pl.when(p != pi)
                def _():
                    stage1(w, p).start()

                @pl.when(p == pi)
                def _():
                    st1[w, pi] = cand[w, pl.ds(r0, SUB)]

                xpad[pl.ds(off, SUB)] = beta * x_p
                xpad[pl.ds(128 + off, SUB)] = -(alpha * x_p)
                hi, lo = split(xpad[...])
                prod = dot(lmat[p // 4], jnp.concatenate([hi, lo], 1))
                coefficients(lax.rem(p + PANELS - 1, PANELS), 1 - b)
                rbuf[...] -= prod[0:256, 0:128] + (prod[0:256, 128:256] + prod[256:512, 0:128])
                xpad[pl.ds(off, SUB)] = jnp.zeros((SUB, 128), F32)
                xpad[pl.ds(128 + off, SUB)] = jnp.zeros((SUB, 128), F32)
            return 0

        lax.fori_loop(0, PANELS // 2, pair, 0)

    def stage1(w, p):
        return pltpu.make_async_remote_copy(
            src_ref=cand.at[w, pl.ds(pl.multiple_of(p * SUB, SUB), SUB)], dst_ref=st1.at[w, pi],
            send_sem=s1s.at[w, p], recv_sem=s1r.at[w, pi],
            device_id=(zlo * 8 + p, col), device_id_type=MESH,
        )

    def stage2(w):
        owner = slots[w] // 2
        for d in range(1, 8):
            src = (pi + d) % 8
            pltpu.make_async_copy(st1.at[w, src], st1.at[w, src], s1r.at[w, src]).wait()
        st2[w, zlo] = pick(st1, w, owner % 8, 8)
        for d in range(1, 4):
            pltpu.make_async_remote_copy(
                src_ref=st2.at[w, zlo], dst_ref=st2.at[w, zlo],
                send_sem=s2s.at[w, d], recv_sem=s2r.at[w, zlo],
                device_id=(((zlo + d) % 4) * 8 + pi, col), device_id_type=MESH,
            ).start()

    def mine():
        return pl.ds(pl.multiple_of(pi * SUB, SUB), SUB)

    def stage3(w):
        owner = slots[w] // 2
        for d in range(1, 4):
            src = (zlo + d) % 4
            pltpu.make_async_copy(st2.at[w, src], st2.at[w, src], s2r.at[w, src]).wait()
        xw[w, mine()] = pick(st2, w, owner // 8, 4)
        for d in range(1, 8):
            pltpu.make_async_remote_copy(
                src_ref=xw.at[w, mine()], dst_ref=xw.at[w, mine()],
                send_sem=s3s.at[w, d], recv_sem=s3r.at[w, pi],
                device_id=(zlo * 8 + (pi + d) % 8, col), device_id_type=MESH,
            ).start()

    def stage4(w):
        for d in range(1, 8):
            src = (pi + d) % 8
            part = xw.at[w, pl.ds(pl.multiple_of(src * SUB, SUB), SUB)]
            pltpu.make_async_copy(part, part, s3r.at[w, src]).wait()

    def drain(w):
        for d in range(1, 8):
            p = (pi + d) % 8
            stage1(w, p).wait_send()
            pltpu.make_async_copy(xw.at[w, mine()], xw.at[w, mine()], s3s.at[w, d]).wait()
        for d in range(1, 4):
            pltpu.make_async_copy(st2.at[w, zlo], st2.at[w, zlo], s2s.at[w, d]).wait()

    def apply(s_cols, t_cols, x):
        lh, ll = split(jnp.concatenate([s_cols, t_cols], 1))
        rh, rl = split(jnp.concatenate([beta * x, -(alpha * x)], 0))
        wide = dot(lh, jnp.concatenate([rh, rl], 1))
        return wide[:, 0:128] + (wide[:, 128:256] + dot(ll, rh))

    order = [col, cp, cm, c2, q, qp, qm, q2]

    def convert(pair, m):
        first, second = order[2 * pair], order[2 * pair + 1]
        rows = pl.ds(m * CH, CH)
        both = jnp.concatenate([zbuf[first, :, rows], zbuf[second, :, rows]], 0)
        hi, lo = split(both.T)
        zhi[rows, 128 * pair:128 * pair + 128] = hi
        zlow[rows, 128 * pair:128 * pair + 128] = lo

    def convert_all(pair):
        def chunk(m, _):
            convert(pair, m)
            return 0

        lax.fori_loop(0, NCH, chunk, 0)

    def gather_x():
        for n, c in enumerate(order):
            at = pl.ds(pl.multiple_of(c * SUB, SUB), SUB)
            for h in range(2):
                hi, lo = split(xw[1 - h, at])
                rows = slice(64 * n + SUB * h, 64 * n + SUB * h + SUB)
                xcat[rows, 0:128] = hi
                xcat[rows, 128:256] = lo

    def product(m):
        rows = pl.ds(m * CH, CH)
        wide = dot(zhi[rows, :], xcat[...])
        out_vec[rows, :] = wide[:, 0:128] + (wide[:, 128:256] + dot(zlow[rows, :], xcat[:, 0:128]))

    right = slice(BLK, 2 * BLK)
    for c in loads[4:7]:
        c.wait()
    pl.semaphore_wait(bar, len(peers))
    send_z(range(Z_A))
    send_own()
    prepare(0)
    coefficients(PANELS - 1, 0)
    solve(0, {})
    stage2(0)
    forward_own(range(0, 4))
    prepare(1)
    coefficients(PANELS - 1, 0)
    stage3(0)
    send_z(range(Z_A, NCH))
    forward_own(range(4, NCH))
    send_far(range(Z_A))
    stage4(0)
    rbuf[...] -= apply(half(s_ref, 1, right), half(t_ref, 1, right), xw[0])
    solve(1, {})
    send_far(range(Z_A, Z_A + 1))
    stage2(1)
    send_far(range(Z_A + 1, Z_A + 2))
    for h in range(2):
        rs = slice(h * BLK, h * BLK + BLK)
        out_side[rs, :] = side_ref[rs, :] - apply(s_ref[rs, BLK:], t_ref[rs, BLK:], xw[0])
    loads[7].wait()
    for k in range(NCH):
        zwait(cp if k % 2 == 0 else cm, k)
    convert_all(0)
    forward_far(range(0, 2))
    send_far(range(Z_A + 2, Z_A + 3))
    for k in range(NCH):
        zwait(c2, k)
    convert_all(1)
    forward_far(range(2, 3))
    stage3(1)
    send_far(range(Z_A + 3, NCH))
    forward_far(range(3, 8))
    early = 2
    for k in range(early):
        zwait(qp if k % 2 == 0 else qm, k)
        zwait(q2, k)
        convert(2, k)
        convert(3, k)
    stage4(1)
    gather_x()
    for h in range(2):
        rs = slice(h * BLK, h * BLK + BLK)
        new = out_side[rs, :] - apply(s_ref[rs, :BLK], t_ref[rs, :BLK], xw[1])
        here = row * 2 + h
        new = jnp.where(jnp.broadcast_to(slots[1] == here, (BLK, 128)), xw[1], new)
        out_side[rs, :] = jnp.where(jnp.broadcast_to(slots[0] == here, (BLK, 128)), xw[0], new)

    for k in range(NCH):
        if k >= early:
            zwait(qp if k % 2 == 0 else qm, k)
            zwait(q2, k)
            convert(2, k)
            convert(3, k)
        product(k)
    for n, (p, k) in enumerate(zsends):
        pltpu.make_async_copy(piece(p, k), piece(p, k), zs.at[n]).wait()
    drain(0)
    drain(1)


def on_device(right_sides, pencil_s, pencil_t, value_alpha, value_beta, selected, block_slot, right_basis, vectors):
    zt = right_basis.transpose(1, 2, 0).reshape(64, ORD)
    vm = pl.BlockSpec(memory_space=pltpu.VMEM)
    dma = pltpu.SemaphoreType.DMA
    sides, prod = pl.pallas_call(
        kernel,
        out_shape=(jax.ShapeDtypeStruct((512, 128), F32), jax.ShapeDtypeStruct((ORD, 128), F32)),
        in_specs=[pl.BlockSpec(memory_space=pltpu.HBM)] * 8,
        out_specs=(vm, vm),
        scratch_shapes=[
            pltpu.VMEM((1, 64), jnp.int32),
            pltpu.VMEM((32, 128), F32),
            pltpu.VMEM((32, 128), F32),
            pltpu.VMEM((1, 128), jnp.int32),
            pltpu.VMEM((512, 128), F32),
            pltpu.VMEM((512, 512), F32),
            pltpu.VMEM((512, 512), F32),
            pltpu.VMEM((8, 64, ORD), F32),
            pltpu.VMEM((ORD, 512), BF),
            pltpu.VMEM((ORD, 512), BF),
            pltpu.VMEM((512, 256), BF),
            pltpu.VMEM((BLK, BLK), F32),
            pltpu.VMEM((BLK, BLK), F32),
            pltpu.VMEM((2, 512, 256), BF),
            pltpu.VMEM((BLK, 128), F32),
            pltpu.VMEM((2, BLK, 128), F32),
            pltpu.VMEM((2, 8, SUB, 128), F32),
            pltpu.VMEM((2, 4, SUB, 128), F32),
            pltpu.VMEM((2, BLK, 128), F32),
            pltpu.VMEM((256, 128), F32),
            pltpu.VMEM((2, SUB, SUB, 128), F32),
            pltpu.VMEM((8, 128), F32),
            dma((8, NCH)), dma((7 * NCH,)),
            dma((2, 8)), dma((2, 8)), dma((2, 4)), dma((2, 4)), dma((2, 8)), dma((2, 8)),
            dma((8,)),
        ],
        compiler_params=pltpu.CompilerParams(
            collective_id=0, has_side_effects=True, vmem_limit_bytes=48 << 20
        ),
    )(
        *(pltpu.with_memory_space_constraint(v, pltpu.HBM) for v in (
            block_slot.reshape(1, 64), value_alpha.reshape(32, 128), value_beta.reshape(32, 128),
            selected.reshape(1, 128), right_sides, pencil_s, pencil_t, zt,
        )),
    )
    return sides, vectors + prod


def solution(mesh):
    return jax.shard_map(
        on_device,
        mesh=mesh,
        in_specs=(
            P("row", "col"), P("row", None), P("row", None), P(), P(), P("col"), P(),
            P("row", None, "col"), P("row", "col"),
        ),
        out_specs=(P("row", "col"), P("row", "col")),
        check_vma=False,
    )
```
